32 devices in a mesh: inp: 16 (over z, y, core), tm: 2 (over x).
Axes of the slice: x: 2, y: 2, z: 4, core: 2. Of those that a mesh axis runs over, the one named last changes fastest.
Arguments:
- samples: bfloat16 [512, 16384], P('inp', 'tm'), may hold values from -6 to 6
- tail: bfloat16 [512, 6144], P('inp'), may hold values from -6 to 6
- taps: float32 [4, 2048], replicated, may hold values from -3 to 3
- tile_table: int32 [16, 4], P('inp'), may hold values from 0 to 3, as said below
Outputs:
- visibilities: float32 [16, 4, 2, 32, 32, 1024], P('inp', None, None, None, None, 'tm')
The draws below stay inside these ranges and needn't reach their ends.
Inputs may be any that keep to these rules, and one draw needn't show every extreme that they name: `tile_table`: each row holds 4 distinct offsets; offsets 0 and 3 both occur.
All inputs are finite; a program needn't handle non-finite values.
Results may differ from the reference program's by a relative error of at most 0.0064.
Values may be sent and summed in bfloat16 or wider, within the bound.
A program may use at most 128 MiB of HBM per device.

```python
import math
import jax
import jax.numpy as jnp
from jax import lax

F = 1024
L = 2048
TAPS = 4
A_DEV = 32
SPAN = 4
TILES_DEV = 4
NBLK = 16
A = 512
SPEC = 8
NT = 16384


def draw_tile_table(key, part):
    scores = jax.random.randint(key, (NBLK, SPAN), 0, 1 << 20) * SPAN + jnp.arange(SPAN, dtype=jnp.int32)[None, :]
    scores = scores.at[0, SPAN - 1].set(-1)
    scores = scores.at[1, 0].set(-1)
    ordering = jnp.argsort(scores, axis=1, stable=True)
    return ordering[:, :TILES_DEV].astype(jnp.int32)


def levels(own_key, shape, split, smallest, high):
    gain = 1.0
    for position, blocks in split:
        draws = jax.random.uniform(jax.random.fold_in(jax.random.fold_in(own_key, 6), position), (blocks,), jnp.float32, smallest / len(split), high / len(split))
        gain = gain * jnp.repeat(jnp.exp(draws), shape[position] // blocks).reshape((-1,) + (1,) * (len(shape) - 1 - position))
    return gain


def gaussian(stream_key, dims, width, limit, shards=(), kind=jnp.bfloat16):
    drawn = jax.random.normal(stream_key, dims, jnp.float32) * width
    if len(shards) > 0:
        drawn = levels(stream_key, dims, shards, -0.22, 0.18) * drawn
    return jnp.clip(drawn, min=-limit, max=limit).astype(kind)


def setup_inputs(seed: int = 0) -> dict:
    splits = jax.random.split(jax.random.key(seed), 5)
    return {
        "samples": gaussian(splits[0], (A, NT), 1.0, 6.0, ((0, 16), (1, 2))),
        "tail": gaussian(splits[1], (A, (TAPS - 1) * L), 1.0, 6.0, ((0, 16),)),
        "taps": gaussian(splits[2], (TAPS, L), 0.5, 3.0, (), jnp.float32),
        "tile_table": draw_tile_table(jax.random.fold_in(splits[4], 71), 0),
    }


def dft_basis():
    sample_rows = jnp.arange(L, dtype=jnp.int32)[:, None]
    channel_cols = jnp.arange(F, dtype=jnp.int32)[None, :]
    angles = (sample_rows * channel_cols % L).astype(jnp.float32) * (2.0 * math.pi / L)
    norm_factor = 1.0 / math.sqrt(L)
    return jnp.concatenate([jnp.cos(angles) * norm_factor, -jnp.sin(angles) * norm_factor], axis=1).astype(jnp.bfloat16)

def correlate(own_block, partner):
    real_own = own_block[:, :, 0, :].astype(jnp.float32)
    imag_own = own_block[:, :, 1, :].astype(jnp.float32)
    real_far = partner[:, :, 0, :].astype(jnp.float32)
    imag_far = partner[:, :, 1, :].astype(jnp.float32)
    high = lax.Precision.HIGHEST
    real_part = jnp.einsum('isc,jsc->ijc', real_own, real_far, precision=high) + jnp.einsum('isc,jsc->ijc', imag_own, imag_far, precision=high)
    imag_part = jnp.einsum('isc,jsc->ijc', imag_own, real_far, precision=high) - jnp.einsum('isc,jsc->ijc', real_own, imag_far, precision=high)
    weight_mean = 1.0 / SPEC
    return jnp.stack([real_part * weight_mean, imag_part * weight_mean], axis=0)

def reference(samples, tail, taps, tile_table):
    basis = dft_basis().astype(jnp.float32)
    stream = jnp.concatenate([samples, tail], axis=1).reshape(NBLK, A_DEV, SPEC + TAPS - 1, L)

    def channelize(block_data):
        frame_data = block_data.astype(jnp.float32)
        filtered = taps[0][None, None, :] * frame_data[:, 0:SPEC, :]
        for tap in range(1, TAPS):
            filtered = filtered + taps[tap][None, None, :] * frame_data[:, tap:tap + SPEC, :]
        filtered = lax.optimization_barrier(filtered.astype(jnp.bfloat16)).astype(jnp.float32)
        spectra = jnp.dot(filtered.reshape(A_DEV * SPEC, L), basis, precision=lax.Precision.HIGHEST, preferred_element_type=jnp.float32)
        return spectra.astype(jnp.bfloat16).reshape(A_DEV, SPEC, 2, F)
    spectra = lax.map(channelize, stream)

    def device_tiles(block_index):
        own_block = lax.dynamic_index_in_dim(spectra, block_index, 0, keepdims=False)

        def single_tile(offset):
            partner_index = ((block_index + offset) % NBLK).astype(jnp.int32)
            partner = lax.dynamic_index_in_dim(spectra, partner_index, 0, keepdims=False)
            return correlate(own_block, partner)
        return lax.map(single_tile, lax.dynamic_index_in_dim(tile_table, block_index, 0, keepdims=False))
    return lax.map(device_tiles, jnp.arange(NBLK, dtype=jnp.int32))
```

```python
import functools
import math

import jax
import jax.numpy as jnp
import numpy as np
from jax import lax
from jax.experimental import pallas as pl
from jax.experimental.pallas import tpu as pltpu
from jax.sharding import PartitionSpec as P

SPAN = 4
LANES = 128
ROWS = 8


def dft_basis(length, parts):
    channels = length // 2
    sample_rows = np.arange(length, dtype=np.int64)[:, None]
    channel_cols = np.arange(channels, dtype=np.int64)[None, :]
    phase_index = sample_rows * channel_cols % length
    table_angles = np.arange(length, dtype=np.float32) * np.float32(2.0 * math.pi / length)
    norm_factor = np.float32(1.0 / math.sqrt(length))
    cosine_table = np.cos(table_angles).astype(np.float32) * norm_factor
    sine_table = -np.sin(table_angles).astype(np.float32) * norm_factor
    both = np.stack([cosine_table[phase_index], sine_table[phase_index]], axis=1)
    both = both.reshape(length, 2, parts, channels // parts).transpose(2, 0, 1, 3)
    return jnp.asarray(both.reshape(parts, length, -1), dtype=jnp.bfloat16)


def channelize_kernel(parts, count, tap_count, length, chunk, where_ref, *refs):
    pieces = refs[:parts]
    tail_ref, taps_ref, basis_ref, out_ref, total, filtered = refs[parts:]
    me = where_ref[0]
    step = pl.program_id(0)
    ants = pieces[0].shape[0]
    cols = lambda frame: pl.ds(pl.multiple_of(frame * length + step * chunk, chunk), chunk)
    taps = [taps_ref[k : k + 1, :] for k in range(tap_count)]
    for part in range(parts):
        at_end = lax.rem(me + part, parts) == parts - 1
        frames = [pieces[part][:, cols(f)] for f in range(count)]
        for f in range(tap_count - 1):
            follower = pieces[(part + 1) % parts][:, cols(f)].astype(jnp.float32)
            closing = tail_ref[:, cols(f)].astype(jnp.float32)
            frames.append(jnp.where(at_end, closing, follower))
        frames = [f.astype(jnp.float32) for f in frames]
        for s in range(count):
            value = taps[0] * frames[s]
            for k in range(1, tap_count):
                value = value + taps[k] * frames[s + k]
            filtered[pl.ds((part * count + s) * ants, ants), :] = value.astype(jnp.bfloat16)

    product = jnp.dot(filtered[...], basis_ref[0], preferred_element_type=jnp.float32)

    @pl.when(step == 0)
    def _():
        total[...] = product

    @pl.when(step > 0)
    def _():
        total[...] += product

    @pl.when(step == pl.num_programs(0) - 1)
    def _():
        out_ref[...] = total[...].astype(jnp.bfloat16)


def channelize(pieces, tail, taps, me):
    parts = len(pieces)
    tap_count, length = taps.shape
    ants, held = pieces[0].shape
    count = held // length
    chunk = length // 4
    basis = dft_basis(length, parts)
    width = basis.shape[2]
    rows = parts * count * ants
    whole = lambda shape: pl.BlockSpec(shape, lambda k, w: (0, 0))
    return pl.pallas_call(
        functools.partial(channelize_kernel, parts, count, tap_count, length, chunk),
        out_shape=jax.ShapeDtypeStruct((rows, width), jnp.bfloat16),
        grid_spec=pltpu.PrefetchScalarGridSpec(
            num_scalar_prefetch=1,
            grid=(length // chunk,),
            in_specs=[whole((ants, held))] * parts
            + [
                whole(tail.shape),
                pl.BlockSpec((tap_count, chunk), lambda k, w: (0, k)),
                pl.BlockSpec((1, chunk, width), lambda k, w: (w[0], k, 0)),
            ],
            out_specs=whole((rows, width)),
            scratch_shapes=[
                pltpu.VMEM((rows, width), jnp.float32),
                pltpu.VMEM((rows, chunk), jnp.bfloat16),
            ],
        ),
        cost_estimate=pl.CostEstimate(
            flops=2 * rows * length * width, bytes_accessed=2 * length * width, transcendentals=0
        ),
        name="channelize",
    )(me.reshape(1), *pieces, tail, taps, basis)


def correlate_kernel(spec_count, first, slot_ref, own_ref, far_ref, *refs):
    out_ref, own_a, own_b, own_ab, far_c, far_s, far_d = refs if first else refs[1:]
    channels = out_ref.shape[-1]
    width = far_ref.shape[1]

    @pl.when(pl.program_id(0) == 0)
    def _():
        for s in range(spec_count):
            real = far_ref[s, :, :channels].astype(jnp.float32)
            imag = far_ref[s, :, channels:].astype(jnp.float32)
            far_c[s] = real
            far_s[s] = real + imag
            far_d[s] = real - imag
            real = own_ref[s, :, :channels].astype(jnp.float32) * (1.0 / spec_count)
            imag = own_ref[s, :, channels:].astype(jnp.float32) * (1.0 / spec_count)
            for group in range(own_a.shape[0]):
                rows = slice(group * ROWS, (group + 1) * ROWS)
                own_a[group, s] = real[rows]
                own_b[group, s] = imag[rows]
                own_ab[group, s] = real[rows] + imag[rows]

    group = pl.program_id(0)

    @pl.loop(0, channels // LANES)
    def _(part):
        lanes = pl.ds(pl.multiple_of(part * LANES, LANES), LANES)
        for pair in range(0, ROWS, 2):
            sums = [[jnp.zeros((width, LANES), jnp.float32) for _ in range(3)] for _ in range(2)]
            for s in range(spec_count):
                c = far_c[s, :, lanes]
                plus = far_s[s, :, lanes]
                minus = far_d[s, :, lanes]
                for i in range(2):
                    row = slice(pair + i, pair + i + 1)
                    sums[i][0] += own_ab[group, s, row, lanes] * c
                    sums[i][1] += own_b[group, s, row, lanes] * minus
                    sums[i][2] += own_a[group, s, row, lanes] * plus
            for i in range(2):
                out_ref[0, 0, pair + i, :, lanes] = sums[i][0] - sums[i][1]
                out_ref[0, 1, pair + i, :, lanes] = sums[i][0] - sums[i][2]


def correlate(own, far, slot, tiles, held):
    spec_count, ants, width = own.shape
    channels = width // 2
    shape = (tiles, 2, ants, ants, channels)
    first = held is None
    inputs = pl.BlockSpec((spec_count, ants, width), lambda i, w: (0, 0, 0))
    return pl.pallas_call(
        functools.partial(correlate_kernel, spec_count, first),
        out_shape=jax.ShapeDtypeStruct(shape, jnp.float32),
        grid_spec=pltpu.PrefetchScalarGridSpec(
            num_scalar_prefetch=1,
            grid=(ants // ROWS,),
            in_specs=[inputs, inputs] + ([] if first else [pl.BlockSpec(memory_space=pl.ANY)]),
            out_specs=pl.BlockSpec(
                (1, 2, ROWS, ants, channels), lambda i, w: (w[0], 0, i, 0, 0)
            ),
            scratch_shapes=[
                pltpu.VMEM((ants // ROWS, spec_count, ROWS, channels), jnp.float32)
            ] * 3
            + [pltpu.VMEM((spec_count, ants, channels), jnp.float32)] * 3,
        ),
        input_output_aliases={} if first else {3: 0},
        cost_estimate=pl.CostEstimate(
            flops=4000000000, bytes_accessed=8 * ants * ants * channels, transcendentals=0
        ),
        name="correlate",
    )(slot.reshape(1), own, far, *([] if first else [held]))


def from_ahead(array, axis, by):
    peers = lax.axis_size(axis)
    return lax.ppermute(array, axis, [((i + by) % peers, i) for i in range(peers)])


def body(samples, tail, taps, tile_table):
    parts = lax.axis_size("tm")
    me = lax.axis_index("tm").astype(jnp.int32)
    pieces = [samples] + [from_ahead(samples, "tm", k) for k in range(1, parts)]
    spectra = channelize(pieces, tail, taps, me)
    ants = samples.shape[0]
    own = spectra.reshape(-1, ants, spectra.shape[1])
    one = from_ahead(own, "inp", 1)
    three = from_ahead(own, "inp", 3)
    peers = lax.axis_size("inp")
    even = lax.rem(lax.axis_index("inp"), 2) == 0
    two = lax.ppermute(
        jnp.where(even, three, one), "inp", [(i, i ^ 1) for i in range(peers)]
    )
    tiles = tile_table.shape[1]
    slots = [jnp.argmax(tile_table[0] == o).astype(jnp.int32) for o in range(SPAN)]
    held = None
    for offset, far in ((0, own), (1, one), (3, three), (2, two)):
        held = correlate(own, far, slots[offset], tiles, held)
    return held[None]


def solution(mesh):
    in_specs = (P("inp", "tm"), P("inp", None), P(), P("inp", None))
    out_specs = P("inp", None, None, None, None, "tm")
    return jax.shard_map(body, mesh=mesh, in_specs=in_specs, out_specs=out_specs, check_vma=False)
```

```python
import functools
import math

import jax
import jax.numpy as jnp
import numpy as np
from jax import lax
from jax.experimental import pallas as pl
from jax.experimental.pallas import tpu as pltpu
from jax.sharding import PartitionSpec as P

LANES = 128
ROWS = 8
STEP = 4
HALF = 16
GRANT = 16 << 20


def dft_basis(length, parts):
    channels = length // 2
    sample_rows = np.arange(length, dtype=np.int64)[:, None]
    channel_cols = np.arange(channels, dtype=np.int64)[None, :]
    phase_index = sample_rows * channel_cols % length
    table_angles = np.arange(length, dtype=np.float32) * np.float32(2.0 * math.pi / length)
    norm_factor = np.float32(1.0 / math.sqrt(length))
    cosine_table = np.cos(table_angles).astype(np.float32) * norm_factor
    sine_table = -np.sin(table_angles).astype(np.float32) * norm_factor
    both = np.stack([cosine_table[phase_index], sine_table[phase_index]], axis=1)
    both = both.reshape(length, 2, parts, channels // parts).transpose(2, 0, 1, 3)
    return jnp.asarray(both.reshape(parts, length, -1), dtype=jnp.bfloat16)


def channelize_kernel(parts, count, tap_count, length, chunk, where_ref, *refs):
    pieces = refs[:parts]
    tail_ref, taps_ref, basis_ref, out_ref, total, filtered = refs[parts:]
    me = where_ref[0]
    step = pl.program_id(0)
    ants = pieces[0].shape[0]
    cols = lambda frame: pl.ds(pl.multiple_of(frame * length + step * chunk, chunk), chunk)
    taps = [taps_ref[k : k + 1, :] for k in range(tap_count)]
    for part in range(parts):
        at_end = lax.rem(me + part, parts) == parts - 1
        frames = [pieces[part][:, cols(f)] for f in range(count)]
        for f in range(tap_count - 1):
            follower = pieces[(part + 1) % parts][:, cols(f)].astype(jnp.float32)
            closing = tail_ref[:, cols(f)].astype(jnp.float32)
            frames.append(jnp.where(at_end, closing, follower))
        frames = [f.astype(jnp.float32) for f in frames]
        for s in range(count):
            value = taps[0] * frames[s]
            for k in range(1, tap_count):
                value = value + taps[k] * frames[s + k]
            filtered[pl.ds((part * count + s) * ants, ants), :] = value.astype(jnp.bfloat16)

    product = jnp.dot(filtered[...], basis_ref[0], preferred_element_type=jnp.float32)

    @pl.when(step == 0)
    def _():
        total[...] = product

    @pl.when(step > 0)
    def _():
        total[...] += product

    @pl.when(step == pl.num_programs(0) - 1)
    def _():
        out_ref[...] = total[...].astype(jnp.bfloat16)


def channelize(pieces, tail, taps, me):
    parts = len(pieces)
    tap_count, length = taps.shape
    ants, held = pieces[0].shape
    count = held // length
    chunk = length // 4
    basis = dft_basis(length, parts)
    width = basis.shape[2]
    rows = parts * count * ants
    whole = lambda shape: pl.BlockSpec(shape, lambda k, w: (0, 0))
    return pl.pallas_call(
        functools.partial(channelize_kernel, parts, count, tap_count, length, chunk),
        out_shape=jax.ShapeDtypeStruct((rows, width), jnp.bfloat16),
        grid_spec=pltpu.PrefetchScalarGridSpec(
            num_scalar_prefetch=1,
            grid=(length // chunk,),
            in_specs=[whole((ants, held))] * parts
            + [
                whole(tail.shape),
                pl.BlockSpec((tap_count, chunk), lambda k, w: (0, k)),
                pl.BlockSpec((1, chunk, width), lambda k, w: (w[0], k, 0)),
            ],
            out_specs=whole((rows, width)),
            scratch_shapes=[
                pltpu.VMEM((rows, width), jnp.float32),
                pltpu.VMEM((rows, chunk), jnp.bfloat16),
            ],
        ),
        cost_estimate=pl.CostEstimate(
            flops=2 * rows * length * width, bytes_accessed=2 * length * width, transcendentals=0
        ),
        compiler_params=pltpu.CompilerParams(vmem_limit_bytes=GRANT),
        name="channelize",
    )(me.reshape(1), *pieces, tail, taps, basis)


def correlate_kernel(spec_count, first, table_ref, own_ref, far_ref, *refs):
    out_ref, own_a, own_b, own_ab, far_c, far_s, far_d = refs if first else refs[1:]
    channels = out_ref.shape[-1]
    width = far_ref.shape[1]

    @pl.when(pl.program_id(0) == 0)
    def _():
        for s in range(spec_count):
            real = far_ref[s, :, :channels].astype(jnp.float32)
            imag = far_ref[s, :, channels:].astype(jnp.float32)
            far_c[s] = real
            far_s[s] = real + imag
            far_d[s] = real - imag
            real = own_ref[s, :, :channels].astype(jnp.float32) * (1.0 / spec_count)
            imag = own_ref[s, :, channels:].astype(jnp.float32) * (1.0 / spec_count)
            for group in range(own_a.shape[0]):
                rows = slice(group * ROWS, (group + 1) * ROWS)
                own_a[group, s] = real[rows]
                own_b[group, s] = imag[rows]
                own_ab[group, s] = real[rows] + imag[rows]

    group = pl.program_id(0)

    for near in range(0, ROWS, STEP):

        @pl.loop(0, channels // LANES)
        def _(part, near=near):
          for half in range(0, width, HALF):
            lanes = pl.ds(pl.multiple_of(part * LANES, LANES), LANES)

            def add(s, sums):
                right = (far_c[s, half : half + HALF, lanes], far_d[s, half : half + HALF, lanes], far_s[s, half : half + HALF, lanes])
                return tuple(
                    total + left[group, s, near + i : near + i + 1, lanes] * right[k]
                    for i in range(STEP)
                    for (k, left), total in zip(
                        enumerate((own_ab, own_b, own_a)), sums[3 * i : 3 * i + 3]
                    )
                )

            zeros = jnp.zeros((HALF, LANES), jnp.float32)
            sums = lax.fori_loop(0, spec_count, add, (zeros,) * (3 * STEP), unroll=4)
            for i in range(STEP):
                out_ref[0, 0, near + i, half : half + HALF, lanes] = sums[3 * i] - sums[3 * i + 1]
                out_ref[0, 1, near + i, half : half + HALF, lanes] = sums[3 * i] - sums[3 * i + 2]


def correlate(own, far, offset, table, held):
    spec_count, ants, width = own.shape
    channels = width // 2
    tiles = table.shape[0]
    slot = lambda w: sum(jnp.where(w[t] == offset, t, 0) for t in range(1, tiles))
    shape = (tiles, 2, ants, ants, channels)
    first = held is None
    inputs = pl.BlockSpec((spec_count, ants, width), lambda i, w: (0, 0, 0))
    return pl.pallas_call(
        functools.partial(correlate_kernel, spec_count, first),
        out_shape=jax.ShapeDtypeStruct(shape, jnp.float32),
        grid_spec=pltpu.PrefetchScalarGridSpec(
            num_scalar_prefetch=1,
            grid=(ants // ROWS,),
            in_specs=[inputs, inputs] + ([] if first else [pl.BlockSpec(memory_space=pl.ANY)]),
            out_specs=pl.BlockSpec(
                (1, 2, ROWS, ants, channels), lambda i, w: (slot(w), 0, i, 0, 0)
            ),
            scratch_shapes=[
                pltpu.VMEM((ants // ROWS, spec_count, ROWS, channels), jnp.float32)
            ] * 3
            + [pltpu.VMEM((spec_count, ants, channels), jnp.float32)] * 3,
        ),
        input_output_aliases={} if first else {3: 0},
        cost_estimate=pl.CostEstimate(
            flops=4000000000, bytes_accessed=8 * ants * ants * channels, transcendentals=0
        ),
        compiler_params=pltpu.CompilerParams(vmem_limit_bytes=GRANT),
        name="correlate",
    )(table, own, far, *([] if first else [held]))


def from_ahead(array, axis, by):
    peers = lax.axis_size(axis)
    return lax.ppermute(array, axis, [((i + by) % peers, i) for i in range(peers)])


def body(samples, tail, taps, tile_table):
    parts = lax.axis_size("tm")
    me = lax.axis_index("tm").astype(jnp.int32)
    pieces = [samples] + [from_ahead(samples, "tm", k) for k in range(1, parts)]
    spectra = channelize(pieces, tail, taps, me)
    ants = samples.shape[0]
    own = spectra.reshape(-1, ants, spectra.shape[1])
    one = from_ahead(own, "inp", 1)
    three = from_ahead(own, "inp", 3)
    peers = lax.axis_size("inp")
    even = lax.rem(lax.axis_index("inp"), 2) == 0
    two = lax.ppermute(
        jnp.where(even, three, one), "inp", [(i, i ^ 1) for i in range(peers)]
    )
    held = None
    for offset, far in ((0, own), (1, one), (3, three), (2, two)):
        held = correlate(own, far, offset, tile_table[0], held)
    return held[None]


def solution(mesh):
    in_specs = (P("inp", "tm"), P("inp", None), P(), P("inp", None))
    out_specs = P("inp", None, None, None, None, "tm")
    return jax.shard_map(body, mesh=mesh, in_specs=in_specs, out_specs=out_specs, check_vma=False)
```

```python
import functools
import math

import jax
import jax.numpy as jnp
import numpy as np
from jax import lax
from jax.experimental import pallas as pl
from jax.experimental.pallas import tpu as pltpu
from jax.sharding import PartitionSpec as P

LANES = 128
ROWS = 8
STEP = 4
HALF = 16
GRANT = 16 << 20


def dft_basis(length, parts):
    channels = length // 2
    sample_rows = np.arange(length, dtype=np.int64)[:, None]
    channel_cols = np.arange(channels, dtype=np.int64)[None, :]
    phase_index = sample_rows * channel_cols % length
    table_angles = np.arange(length, dtype=np.float32) * np.float32(2.0 * math.pi / length)
    norm_factor = np.float32(1.0 / math.sqrt(length))
    cosine_table = np.cos(table_angles).astype(np.float32) * norm_factor
    sine_table = -np.sin(table_angles).astype(np.float32) * norm_factor
    both = np.stack([cosine_table[phase_index], sine_table[phase_index]], axis=1)
    both = both.reshape(length, 2, parts, channels // parts).transpose(2, 0, 1, 3)
    return jnp.asarray(both.reshape(parts, length, -1), dtype=jnp.bfloat16)


def channelize_kernel(parts, count, tap_count, length, chunk, where_ref, *refs):
    pieces = refs[:parts]
    tail_ref, taps_ref, basis_ref, out_ref, total, filtered = refs[parts:]
    me = where_ref[0]
    step = pl.program_id(0)
    ants = pieces[0].shape[0]
    cols = lambda frame: pl.ds(pl.multiple_of(frame * length + step * chunk, chunk), chunk)
    taps = [taps_ref[k : k + 1, :] for k in range(tap_count)]
    for part in range(parts):
        at_end = lax.rem(me + part, parts) == parts - 1
        frames = [pieces[part][:, cols(f)] for f in range(count)]
        for f in range(tap_count - 1):
            follower = pieces[(part + 1) % parts][:, cols(f)].astype(jnp.float32)
            closing = tail_ref[:, cols(f)].astype(jnp.float32)
            frames.append(jnp.where(at_end, closing, follower))
        frames = [f.astype(jnp.float32) for f in frames]
        for s in range(count):
            value = taps[0] * frames[s]
            for k in range(1, tap_count):
                value = value + taps[k] * frames[s + k]
            filtered[pl.ds((part * count + s) * ants, ants), :] = value.astype(jnp.bfloat16)

    product = jnp.dot(filtered[...], basis_ref[...], preferred_element_type=jnp.float32)

    @pl.when(step == 0)
    def _():
        total[...] = product

    @pl.when(step > 0)
    def _():
        total[...] += product

    @pl.when(step == pl.num_programs(0) - 1)
    def _():
        out_ref[...] = total[...].astype(jnp.bfloat16)


def channelize(pieces, tail, taps, me):
    parts = len(pieces)
    tap_count, length = taps.shape
    ants, held = pieces[0].shape
    count = held // length
    chunk = length // 4
    basis = lax.dynamic_index_in_dim(dft_basis(length, parts), me, 0, keepdims=False)
    width = basis.shape[1]
    rows = parts * count * ants
    whole = lambda shape: pl.BlockSpec(shape, lambda k, w: (0, 0))
    return pl.pallas_call(
        functools.partial(channelize_kernel, parts, count, tap_count, length, chunk),
        out_shape=jax.ShapeDtypeStruct((rows, width), jnp.bfloat16),
        grid_spec=pltpu.PrefetchScalarGridSpec(
            num_scalar_prefetch=1,
            grid=(length // chunk,),
            in_specs=[whole((ants, held))] * parts
            + [
                whole(tail.shape),
                pl.BlockSpec((tap_count, chunk), lambda k, w: (0, k)),
                pl.BlockSpec((chunk, width), lambda k, w: (k, 0)),
            ],
            out_specs=whole((rows, width)),
            scratch_shapes=[
                pltpu.VMEM((rows, width), jnp.float32),
                pltpu.VMEM((rows, chunk), jnp.bfloat16),
            ],
        ),
        cost_estimate=pl.CostEstimate(
            flops=2 * rows * length * width, bytes_accessed=2 * length * width, transcendentals=0
        ),
        compiler_params=pltpu.CompilerParams(vmem_limit_bytes=GRANT),
        name="channelize",
    )(me.reshape(1), *pieces, tail, taps, basis)


def correlate_kernel(spec_count, first, table_ref, own_ref, far_ref, *refs):
    out_ref, own_a, own_b, own_ab, far_c, far_s, far_d = refs if first else refs[1:]
    channels = out_ref.shape[-1]
    width = far_ref.shape[1]

    @pl.when(pl.program_id(0) == 0)
    def _():
        for s in range(spec_count):
            real = far_ref[s, :, :channels].astype(jnp.float32)
            imag = far_ref[s, :, channels:].astype(jnp.float32)
            far_c[s] = real
            far_s[s] = real + imag
            far_d[s] = real - imag
            real = own_ref[s, :, :channels].astype(jnp.float32) * (1.0 / spec_count)
            imag = own_ref[s, :, channels:].astype(jnp.float32) * (1.0 / spec_count)
            for group in range(own_a.shape[0]):
                rows = slice(group * ROWS, (group + 1) * ROWS)
                own_a[group, s] = real[rows]
                own_b[group, s] = imag[rows]
                own_ab[group, s] = real[rows] + imag[rows]

    group = pl.program_id(0)

    for near in range(0, ROWS, STEP):

        @pl.loop(0, channels // LANES)
        def _(part, near=near):
            lanes = pl.ds(pl.multiple_of(part * LANES, LANES), LANES)
            for half in range(0, width, HALF):
                some = slice(half, half + HALF)

                def add(s, sums):
                    right = [f[s, some, lanes] for f in (far_c, far_d, far_s)]
                    return tuple(
                        total + left[group, s, near + i : near + i + 1, lanes] * right[k]
                        for i in range(STEP)
                        for (k, left), total in zip(
                            enumerate((own_ab, own_b, own_a)), sums[3 * i : 3 * i + 3]
                        )
                    )

                zeros = jnp.zeros((HALF, LANES), jnp.float32)
                sums = lax.fori_loop(0, spec_count, add, (zeros,) * (3 * STEP), unroll=4)
                for i in range(STEP):
                    out_ref[0, 0, near + i, some, lanes] = sums[3 * i] - sums[3 * i + 1]
                    out_ref[0, 1, near + i, some, lanes] = sums[3 * i] - sums[3 * i + 2]


def correlate(own, far, offset, table, held):
    spec_count, ants, width = own.shape
    channels = width // 2
    tiles = table.shape[0]
    slot = lambda w: sum(jnp.where(w[t] == offset, t, 0) for t in range(1, tiles))
    shape = (tiles, 2, ants, ants, channels)
    first = held is None
    inputs = pl.BlockSpec((spec_count, ants, width), lambda i, w: (0, 0, 0))
    return pl.pallas_call(
        functools.partial(correlate_kernel, spec_count, first),
        out_shape=jax.ShapeDtypeStruct(shape, jnp.float32),
        grid_spec=pltpu.PrefetchScalarGridSpec(
            num_scalar_prefetch=1,
            grid=(ants // ROWS,),
            in_specs=[inputs, inputs] + ([] if first else [pl.BlockSpec(memory_space=pl.ANY)]),
            out_specs=pl.BlockSpec(
                (1, 2, ROWS, ants, channels), lambda i, w: (slot(w), 0, i, 0, 0)
            ),
            scratch_shapes=[
                pltpu.VMEM((ants // ROWS, spec_count, ROWS, channels), jnp.float32)
            ] * 3
            + [pltpu.VMEM((spec_count, ants, channels), jnp.float32)] * 3,
        ),
        input_output_aliases={} if first else {3: 0},
        cost_estimate=pl.CostEstimate(
            flops=4000000000, bytes_accessed=8 * ants * ants * channels, transcendentals=0
        ),
        compiler_params=pltpu.CompilerParams(vmem_limit_bytes=GRANT),
        name="correlate",
    )(table, own, far, *([] if first else [held]))


def from_ahead(array, axis, by):
    peers = lax.axis_size(axis)
    return lax.ppermute(array, axis, [((i + by) % peers, i) for i in range(peers)])


def body(samples, tail, taps, tile_table):
    parts = lax.axis_size("tm")
    me = lax.axis_index("tm").astype(jnp.int32)
    pieces = [samples] + [from_ahead(samples, "tm", k) for k in range(1, parts)]
    spectra = channelize(pieces, tail, taps, me)
    ants = samples.shape[0]
    own = spectra.reshape(-1, ants, spectra.shape[1])
    one = from_ahead(own, "inp", 1)
    three = from_ahead(own, "inp", 3)
    held = correlate(own, own, 0, tile_table[0], None)
    held = correlate(own, one, 1, tile_table[0], held)
    three, held = lax.optimization_barrier((three, held))
    peers = lax.axis_size("inp")
    even = lax.rem(lax.axis_index("inp"), 2) == 0
    two = lax.ppermute(
        jnp.where(even, three, one), "inp", [(i, i ^ 1) for i in range(peers)]
    )
    held = correlate(own, three, 3, tile_table[0], held)
    held = correlate(own, two, 2, tile_table[0], held)
    return held[None]


def solution(mesh):
    in_specs = (P("inp", "tm"), P("inp", None), P(), P("inp", None))
    out_specs = P("inp", None, None, None, None, "tm")
    return jax.shard_map(body, mesh=mesh, in_specs=in_specs, out_specs=out_specs, check_vma=False)
```

```python
import functools
import math

import jax
import jax.numpy as jnp
import numpy as np
from jax import lax
from jax.experimental import pallas as pl
from jax.experimental.pallas import tpu as pltpu
from jax.sharding import PartitionSpec as P

LANES = 128
ROWS = 8
STEP = 4
HALF = 16
GRANT = 16 << 20


def dft_basis(length, parts):
    channels = length // 2
    sample_rows = np.arange(length, dtype=np.int64)[:, None]
    channel_cols = np.arange(channels, dtype=np.int64)[None, :]
    phase_index = sample_rows * channel_cols % length
    table_angles = np.arange(length, dtype=np.float32) * np.float32(2.0 * math.pi / length)
    norm_factor = np.float32(1.0 / math.sqrt(length))
    cosine_table = np.cos(table_angles).astype(np.float32) * norm_factor
    sine_table = -np.sin(table_angles).astype(np.float32) * norm_factor
    both = np.stack([cosine_table[phase_index], sine_table[phase_index]], axis=1)
    both = both.reshape(length, 2, parts, channels // parts).transpose(2, 0, 1, 3)
    return jnp.asarray(both.reshape(parts, length, -1), dtype=jnp.bfloat16)


def channelize_kernel(parts, count, tap_count, length, chunk, where_ref, *refs):
    pieces = refs[:parts]
    taps_ref, basis_ref, out_ref, total, filtered = refs[parts:]
    me = where_ref[0]
    step = pl.program_id(0)
    ants = pieces[0].shape[0]
    cols = lambda frame: pl.ds(pl.multiple_of(frame * length + step * chunk, chunk), chunk)
    taps = [taps_ref[k : k + 1, :] for k in range(tap_count)]
    for part in range(parts):
        at_end = lax.rem(me + part, parts) == parts - 1
        frames = [pieces[part][:, cols(f)] for f in range(count)]
        for f in range(tap_count - 1):
            follower = pieces[(part + 1) % parts][:, cols(f)].astype(jnp.float32)
            closing = pieces[0][:, cols(count + f)].astype(jnp.float32)
            frames.append(jnp.where(at_end, closing, follower))
        frames = [f.astype(jnp.float32) for f in frames]
        for s in range(count):
            value = taps[0] * frames[s]
            for k in range(1, tap_count):
                value = value + taps[k] * frames[s + k]
            filtered[pl.ds((part * count + s) * ants, ants), :] = value.astype(jnp.bfloat16)

    product = jnp.dot(filtered[...], basis_ref[...], preferred_element_type=jnp.float32)

    @pl.when(step == 0)
    def _():
        total[...] = product

    @pl.when(step > 0)
    def _():
        total[...] += product

    @pl.when(step == pl.num_programs(0) - 1)
    def _():
        out_ref[...] = total[...].astype(jnp.bfloat16)


def channelize(pieces, tail, taps, me):
    parts = len(pieces)
    tap_count, length = taps.shape
    ants, held = pieces[0].shape
    count = held // length
    chunk = length // 4
    basis = lax.dynamic_index_in_dim(dft_basis(length, parts), me, 0, keepdims=False)
    width = basis.shape[1]
    rows = parts * count * ants
    first = jnp.concatenate([pieces[0], tail], axis=1)
    doubled = jnp.concatenate([taps, taps], axis=0)
    whole = lambda shape: pl.BlockSpec(shape, lambda k, w: (0, 0))
    return pl.pallas_call(
        functools.partial(channelize_kernel, parts, count, tap_count, length, chunk),
        out_shape=jax.ShapeDtypeStruct((rows, width), jnp.bfloat16),
        grid_spec=pltpu.PrefetchScalarGridSpec(
            num_scalar_prefetch=1,
            grid=(length // chunk,),
            in_specs=[whole(first.shape)]
            + [whole((ants, held))] * (parts - 1)
            + [
                pl.BlockSpec((2 * tap_count, chunk), lambda k, w: (0, k)),
                pl.BlockSpec((chunk, width), lambda k, w: (k, 0)),
            ],
            out_specs=whole((rows, width)),
            scratch_shapes=[
                pltpu.VMEM((rows, width), jnp.float32),
                pltpu.VMEM((rows, chunk), jnp.bfloat16),
            ],
        ),
        cost_estimate=pl.CostEstimate(
            flops=2 * rows * length * width, bytes_accessed=2 * length * width, transcendentals=0
        ),
        compiler_params=pltpu.CompilerParams(vmem_limit_bytes=GRANT),
        name="channelize",
    )(me.reshape(1), first, *pieces[1:], doubled, basis)


def correlate_kernel(spec_count, first, table_ref, own_ref, far_ref, *refs):
    out_ref, own_a, own_b, own_ab, far_c, far_s, far_d = refs if first else refs[1:]
    channels = out_ref.shape[-1]
    width = far_ref.shape[1]

    @pl.when(pl.program_id(0) == 0)
    def _():
        for s in range(spec_count):
            real = far_ref[s, :, :channels].astype(jnp.float32)
            imag = far_ref[s, :, channels:].astype(jnp.float32)
            far_c[s] = real
            far_s[s] = real + imag
            far_d[s] = real - imag
            real = own_ref[s, :, :channels].astype(jnp.float32) * (1.0 / spec_count)
            imag = own_ref[s, :, channels:].astype(jnp.float32) * (1.0 / spec_count)
            for group in range(own_a.shape[0]):
                rows = slice(group * ROWS, (group + 1) * ROWS)
                own_a[group, s] = real[rows]
                own_b[group, s] = imag[rows]
                own_ab[group, s] = real[rows] + imag[rows]

    group = pl.program_id(0)

    for near in range(0, ROWS, STEP):

        @pl.loop(0, channels // LANES)
        def _(part, near=near):
            lanes = pl.ds(pl.multiple_of(part * LANES, LANES), LANES)
            for half in range(0, width, HALF):
                some = slice(half, half + HALF)

                def add(s, sums):
                    right = [f[s, some, lanes] for f in (far_c, far_d, far_s)]
                    return tuple(
                        total + left[group, s, near + i : near + i + 1, lanes] * right[k]
                        for i in range(STEP)
                        for (k, left), total in zip(
                            enumerate((own_ab, own_b, own_a)), sums[3 * i : 3 * i + 3]
                        )
                    )

                zeros = jnp.zeros((HALF, LANES), jnp.float32)
                sums = lax.fori_loop(0, spec_count, add, (zeros,) * (3 * STEP), unroll=4)
                for i in range(STEP):
                    out_ref[0, 0, near + i, some, lanes] = sums[3 * i] - sums[3 * i + 1]
                    out_ref[0, 1, near + i, some, lanes] = sums[3 * i] - sums[3 * i + 2]


def correlate(own, far, offset, table, held):
    spec_count, ants, width = own.shape
    channels = width // 2
    tiles = table.shape[0]
    slot = lambda w: sum(jnp.where(w[t] == offset, t, 0) for t in range(1, tiles))
    shape = (tiles, 2, ants, ants, channels)
    first = held is None
    inputs = pl.BlockSpec((spec_count, ants, width), lambda i, w: (0, 0, 0))
    return pl.pallas_call(
        functools.partial(correlate_kernel, spec_count, first),
        out_shape=jax.ShapeDtypeStruct(shape, jnp.float32),
        grid_spec=pltpu.PrefetchScalarGridSpec(
            num_scalar_prefetch=1,
            grid=(ants // ROWS,),
            in_specs=[inputs, inputs] + ([] if first else [pl.BlockSpec(memory_space=pl.ANY)]),
            out_specs=pl.BlockSpec(
                (1, 2, ROWS, ants, channels), lambda i, w: (slot(w), 0, i, 0, 0)
            ),
            scratch_shapes=[
                pltpu.VMEM((ants // ROWS, spec_count, ROWS, channels), jnp.float32)
            ] * 3
            + [pltpu.VMEM((spec_count, ants, channels), jnp.float32)] * 3,
        ),
        input_output_aliases={} if first else {3: 0},
        cost_estimate=pl.CostEstimate(
            flops=4000000000, bytes_accessed=8 * ants * ants * channels, transcendentals=0
        ),
        compiler_params=pltpu.CompilerParams(vmem_limit_bytes=GRANT),
        name="correlate",
    )(table, own, far, *([] if first else [held]))


def from_ahead(array, axis, by):
    peers = lax.axis_size(axis)
    return lax.ppermute(array, axis, [((i + by) % peers, i) for i in range(peers)])


def body(samples, tail, taps, tile_table):
    parts = lax.axis_size("tm")
    me = lax.axis_index("tm").astype(jnp.int32)
    pieces = [samples] + [from_ahead(samples, "tm", k) for k in range(1, parts)]
    spectra = channelize(pieces, tail, taps, me)
    ants = samples.shape[0]
    own = spectra.reshape(-1, ants, spectra.shape[1])
    one = from_ahead(own, "inp", 1)
    three = from_ahead(own, "inp", 3)
    held = correlate(own, own, 0, tile_table[0], None)
    held = correlate(own, one, 1, tile_table[0], held)
    three, held = lax.optimization_barrier((three, held))
    peers = lax.axis_size("inp")
    even = lax.rem(lax.axis_index("inp"), 2) == 0
    two = lax.ppermute(
        jnp.where(even, three, one), "inp", [(i, i ^ 1) for i in range(peers)]
    )
    held = correlate(own, three, 3, tile_table[0], held)
    held = correlate(own, two, 2, tile_table[0], held)
    return held[None]


def solution(mesh):
    in_specs = (P("inp", "tm"), P("inp", None), P(), P("inp", None))
    out_specs = P("inp", None, None, None, None, "tm")
    return jax.shard_map(body, mesh=mesh, in_specs=in_specs, out_specs=out_specs, check_vma=False)
```

```python
import functools
import math

import jax
import jax.numpy as jnp
import numpy as np
from jax import lax
from jax.experimental import pallas as pl
from jax.experimental.pallas import tpu as pltpu
from jax.sharding import PartitionSpec as P

LANES = 128
ROWS = 4
STEP = 4
HALF = 16
GRANT = 16 << 20


def dft_basis(length, parts):
    channels = length // 2
    sample_rows = np.arange(length, dtype=np.int64)[:, None]
    channel_cols = np.arange(channels, dtype=np.int64)[None, :]
    phase_index = sample_rows * channel_cols % length
    table_angles = np.arange(length, dtype=np.float32) * np.float32(2.0 * math.pi / length)
    norm_factor = np.float32(1.0 / math.sqrt(length))
    cosine_table = np.cos(table_angles).astype(np.float32) * norm_factor
    sine_table = -np.sin(table_angles).astype(np.float32) * norm_factor
    both = np.stack([cosine_table[phase_index], sine_table[phase_index]], axis=1)
    both = both.reshape(length, 2, parts, channels // parts).transpose(2, 0, 1, 3)
    return jnp.asarray(both.reshape(parts, length, -1), dtype=jnp.bfloat16)


def channelize_kernel(parts, count, tap_count, length, chunk, where_ref, *refs):
    pieces = refs[:parts]
    taps_ref, basis_ref, out_ref, total, filtered = refs[parts:]
    me = where_ref[0]
    step = pl.program_id(0)
    ants = pieces[0].shape[0]
    cols = lambda frame: pl.ds(pl.multiple_of(frame * length + step * chunk, chunk), chunk)
    taps = [taps_ref[k : k + 1, :] for k in range(tap_count)]
    for part in range(parts):
        at_end = lax.rem(me + part, parts) == parts - 1
        frames = [pieces[part][:, cols(f)] for f in range(count)]
        for f in range(tap_count - 1):
            follower = pieces[(part + 1) % parts][:, cols(f)].astype(jnp.float32)
            closing = pieces[0][:, cols(count + f)].astype(jnp.float32)
            frames.append(jnp.where(at_end, closing, follower))
        frames = [f.astype(jnp.float32) for f in frames]
        for s in range(count):
            value = taps[0] * frames[s]
            for k in range(1, tap_count):
                value = value + taps[k] * frames[s + k]
            filtered[pl.ds((part * count + s) * ants, ants), :] = value.astype(jnp.bfloat16)

    product = jnp.dot(filtered[...], basis_ref[...], preferred_element_type=jnp.float32)

    @pl.when(step == 0)
    def _():
        total[...] = product

    @pl.when(step > 0)
    def _():
        total[...] += product

    @pl.when(step == pl.num_programs(0) - 1)
    def _():
        out_ref[...] = total[...].astype(jnp.bfloat16)


def channelize(pieces, tail, taps, me):
    parts = len(pieces)
    tap_count, length = taps.shape
    ants, held = pieces[0].shape
    count = held // length
    chunk = length // 4
    basis = lax.dynamic_index_in_dim(dft_basis(length, parts), me, 0, keepdims=False)
    width = basis.shape[1]
    rows = parts * count * ants
    first = jnp.concatenate([pieces[0], tail], axis=1)
    doubled = jnp.concatenate([taps, taps], axis=0)
    whole = lambda shape: pl.BlockSpec(shape, lambda k, w: (0, 0))
    return pl.pallas_call(
        functools.partial(channelize_kernel, parts, count, tap_count, length, chunk),
        out_shape=jax.ShapeDtypeStruct((rows, width), jnp.bfloat16),
        grid_spec=pltpu.PrefetchScalarGridSpec(
            num_scalar_prefetch=1,
            grid=(length // chunk,),
            in_specs=[whole(first.shape)]
            + [whole((ants, held))] * (parts - 1)
            + [
                pl.BlockSpec((2 * tap_count, chunk), lambda k, w: (0, k)),
                pl.BlockSpec((chunk, width), lambda k, w: (k, 0)),
            ],
            out_specs=whole((rows, width)),
            scratch_shapes=[
                pltpu.VMEM((rows, width), jnp.float32),
                pltpu.VMEM((rows, chunk), jnp.bfloat16),
            ],
        ),
        cost_estimate=pl.CostEstimate(
            flops=2 * rows * length * width, bytes_accessed=2 * length * width, transcendentals=0
        ),
        compiler_params=pltpu.CompilerParams(vmem_limit_bytes=GRANT),
        name="channelize",
    )(me.reshape(1), first, *pieces[1:], doubled, basis)


def correlate_kernel(spec_count, first, table_ref, own_ref, far_ref, *refs):
    out_ref, own_a, own_b, own_ab, far_c, far_s, far_d = refs if first else refs[1:]
    channels = out_ref.shape[-1]
    width = far_ref.shape[1]

    @pl.when(pl.program_id(0) == 0)
    def _():
        for s in range(spec_count):
            real = far_ref[s, :, :channels].astype(jnp.float32)
            imag = far_ref[s, :, channels:].astype(jnp.float32)
            far_c[s] = real
            far_s[s] = real + imag
            far_d[s] = real - imag
            real = own_ref[s, :, :channels].astype(jnp.float32) * (1.0 / spec_count)
            imag = own_ref[s, :, channels:].astype(jnp.float32) * (1.0 / spec_count)
            for group in range(own_a.shape[0]):
                rows = slice(group * ROWS, (group + 1) * ROWS)
                own_a[group, s] = real[rows]
                own_b[group, s] = imag[rows]
                own_ab[group, s] = real[rows] + imag[rows]

    group = pl.program_id(0)

    for near in range(0, ROWS, STEP):

        @pl.loop(0, channels // LANES)
        def _(part, near=near):
            lanes = pl.ds(pl.multiple_of(part * LANES, LANES), LANES)
            for half in range(0, width, HALF):
                some = slice(half, half + HALF)

                def add(s, sums):
                    right = [f[s, some, lanes] for f in (far_c, far_d, far_s)]
                    return tuple(
                        total + left[group, s, near + i : near + i + 1, lanes] * right[k]
                        for i in range(STEP)
                        for (k, left), total in zip(
                            enumerate((own_ab, own_b, own_a)), sums[3 * i : 3 * i + 3]
                        )
                    )

                zeros = jnp.zeros((HALF, LANES), jnp.float32)
                sums = lax.fori_loop(0, spec_count, add, (zeros,) * (3 * STEP), unroll=4)
                for i in range(STEP):
                    out_ref[0, 0, near + i, some, lanes] = sums[3 * i] - sums[3 * i + 1]
                    out_ref[0, 1, near + i, some, lanes] = sums[3 * i] - sums[3 * i + 2]


def correlate(own, far, offset, table, held):
    spec_count, ants, width = own.shape
    channels = width // 2
    tiles = table.shape[0]
    slot = lambda w: sum(jnp.where(w[t] == offset, t, 0) for t in range(1, tiles))
    shape = (tiles, 2, ants, ants, channels)
    first = held is None
    inputs = pl.BlockSpec((spec_count, ants, width), lambda i, w: (0, 0, 0))
    return pl.pallas_call(
        functools.partial(correlate_kernel, spec_count, first),
        out_shape=jax.ShapeDtypeStruct(shape, jnp.float32),
        grid_spec=pltpu.PrefetchScalarGridSpec(
            num_scalar_prefetch=1,
            grid=(ants // ROWS,),
            in_specs=[inputs, inputs] + ([] if first else [pl.BlockSpec(memory_space=pl.ANY)]),
            out_specs=pl.BlockSpec(
                (1, 2, ROWS, ants, channels), lambda i, w: (slot(w), 0, i, 0, 0)
            ),
            scratch_shapes=[
                pltpu.VMEM((ants // ROWS, spec_count, ROWS, channels), jnp.float32)
            ] * 3
            + [pltpu.VMEM((spec_count, ants, channels), jnp.float32)] * 3,
        ),
        input_output_aliases={} if first else {3: 0},
        cost_estimate=pl.CostEstimate(
            flops=4000000000, bytes_accessed=8 * ants * ants * channels, transcendentals=0
        ),
        compiler_params=pltpu.CompilerParams(vmem_limit_bytes=GRANT),
        name="correlate",
    )(table, own, far, *([] if first else [held]))


def from_ahead(array, axis, by):
    peers = lax.axis_size(axis)
    return lax.ppermute(array, axis, [((i + by) % peers, i) for i in range(peers)])


def body(samples, tail, taps, tile_table):
    parts = lax.axis_size("tm")
    me = lax.axis_index("tm").astype(jnp.int32)
    pieces = [samples] + [from_ahead(samples, "tm", k) for k in range(1, parts)]
    spectra = channelize(pieces, tail, taps, me)
    ants = samples.shape[0]
    own = spectra.reshape(-1, ants, spectra.shape[1])
    one = from_ahead(own, "inp", 1)
    three = from_ahead(own, "inp", 3)
    held = correlate(own, own, 0, tile_table[0], None)
    held = correlate(own, one, 1, tile_table[0], held)
    three, held = lax.optimization_barrier((three, held))
    peers = lax.axis_size("inp")
    even = lax.rem(lax.axis_index("inp"), 2) == 0
    two = lax.ppermute(
        jnp.where(even, three, one), "inp", [(i, i ^ 1) for i in range(peers)]
    )
    held = correlate(own, three, 3, tile_table[0], held)
    held = correlate(own, two, 2, tile_table[0], held)
    return held[None]


def solution(mesh):
    in_specs = (P("inp", "tm"), P("inp", None), P(), P("inp", None))
    out_specs = P("inp", None, None, None, None, "tm")
    return jax.shard_map(body, mesh=mesh, in_specs=in_specs, out_specs=out_specs, check_vma=False)
```

```python
import functools
import math

import jax
import jax.numpy as jnp
import numpy as np
from jax import lax
from jax.experimental import pallas as pl
from jax.experimental.pallas import tpu as pltpu
from jax.sharding import PartitionSpec as P

LANES = 128
ROWS = 16
STEP = 4
HALF = 16
GRANT = 16 << 20


def dft_basis(length, parts):
    channels = length // 2
    sample_rows = np.arange(length, dtype=np.int64)[:, None]
    channel_cols = np.arange(channels, dtype=np.int64)[None, :]
    phase_index = sample_rows * channel_cols % length
    table_angles = np.arange(length, dtype=np.float32) * np.float32(2.0 * math.pi / length)
    norm_factor = np.float32(1.0 / math.sqrt(length))
    cosine_table = np.cos(table_angles).astype(np.float32) * norm_factor
    sine_table = -np.sin(table_angles).astype(np.float32) * norm_factor
    both = np.stack([cosine_table[phase_index], sine_table[phase_index]], axis=1)
    both = both.reshape(length, 2, parts, channels // parts).transpose(2, 0, 1, 3)
    return jnp.asarray(both.reshape(parts, length, -1), dtype=jnp.bfloat16)


def channelize_kernel(parts, count, tap_count, length, chunk, where_ref, *refs):
    pieces = refs[:parts]
    taps_ref, basis_ref, out_ref, total, filtered = refs[parts:]
    me = where_ref[0]
    step = pl.program_id(0)
    ants = pieces[0].shape[0]
    cols = lambda frame: pl.ds(pl.multiple_of(frame * length + step * chunk, chunk), chunk)
    taps = [taps_ref[k : k + 1, :] for k in range(tap_count)]
    for part in range(parts):
        at_end = lax.rem(me + part, parts) == parts - 1
        frames = [pieces[part][:, cols(f)] for f in range(count)]
        for f in range(tap_count - 1):
            follower = pieces[(part + 1) % parts][:, cols(f)].astype(jnp.float32)
            closing = pieces[0][:, cols(count + f)].astype(jnp.float32)
            frames.append(jnp.where(at_end, closing, follower))
        frames = [f.astype(jnp.float32) for f in frames]
        for s in range(count):
            value = taps[0] * frames[s]
            for k in range(1, tap_count):
                value = value + taps[k] * frames[s + k]
            filtered[pl.ds((part * count + s) * ants, ants), :] = value.astype(jnp.bfloat16)

    product = jnp.dot(filtered[...], basis_ref[...], preferred_element_type=jnp.float32)

    @pl.when(step == 0)
    def _():
        total[...] = product

    @pl.when(step > 0)
    def _():
        total[...] += product

    @pl.when(step == pl.num_programs(0) - 1)
    def _():
        out_ref[...] = total[...].astype(jnp.bfloat16)


def channelize(pieces, tail, taps, me):
    parts = len(pieces)
    tap_count, length = taps.shape
    ants, held = pieces[0].shape
    count = held // length
    chunk = length // 4
    basis = lax.dynamic_index_in_dim(dft_basis(length, parts), me, 0, keepdims=False)
    width = basis.shape[1]
    rows = parts * count * ants
    first = jnp.concatenate([pieces[0], tail], axis=1)
    doubled = jnp.concatenate([taps, taps], axis=0)
    whole = lambda shape: pl.BlockSpec(shape, lambda k, w: (0, 0))
    return pl.pallas_call(
        functools.partial(channelize_kernel, parts, count, tap_count, length, chunk),
        out_shape=jax.ShapeDtypeStruct((rows, width), jnp.bfloat16),
        grid_spec=pltpu.PrefetchScalarGridSpec(
            num_scalar_prefetch=1,
            grid=(length // chunk,),
            in_specs=[whole(first.shape)]
            + [whole((ants, held))] * (parts - 1)
            + [
                pl.BlockSpec((2 * tap_count, chunk), lambda k, w: (0, k)),
                pl.BlockSpec((chunk, width), lambda k, w: (k, 0)),
            ],
            out_specs=whole((rows, width)),
            scratch_shapes=[
                pltpu.VMEM((rows, width), jnp.float32),
                pltpu.VMEM((rows, chunk), jnp.bfloat16),
            ],
        ),
        cost_estimate=pl.CostEstimate(
            flops=2 * rows * length * width, bytes_accessed=2 * length * width, transcendentals=0
        ),
        compiler_params=pltpu.CompilerParams(vmem_limit_bytes=GRANT),
        name="channelize",
    )(me.reshape(1), first, *pieces[1:], doubled, basis)


def correlate_kernel(spec_count, first, table_ref, own_ref, far_ref, *refs):
    out_ref, own_a, own_b, own_ab, far_c, far_s, far_d = refs if first else refs[1:]
    channels = out_ref.shape[-1]
    width = far_ref.shape[1]

    @pl.when(pl.program_id(0) == 0)
    def _():
        for s in range(spec_count):
            real = far_ref[s, :, :channels].astype(jnp.float32)
            imag = far_ref[s, :, channels:].astype(jnp.float32)
            far_c[s] = real
            far_s[s] = real + imag
            far_d[s] = real - imag
            real = own_ref[s, :, :channels].astype(jnp.float32) * (1.0 / spec_count)
            imag = own_ref[s, :, channels:].astype(jnp.float32) * (1.0 / spec_count)
            for group in range(own_a.shape[0]):
                rows = slice(group * ROWS, (group + 1) * ROWS)
                own_a[group, s] = real[rows]
                own_b[group, s] = imag[rows]
                own_ab[group, s] = real[rows] + imag[rows]

    group = pl.program_id(0)

    for near in range(0, ROWS, STEP):

        @pl.loop(0, channels // LANES)
        def _(part, near=near):
            lanes = pl.ds(pl.multiple_of(part * LANES, LANES), LANES)
            for half in range(0, width, HALF):
                some = slice(half, half + HALF)

                def add(s, sums):
                    right = [f[s, some, lanes] for f in (far_c, far_d, far_s)]
                    return tuple(
                        total + left[group, s, near + i : near + i + 1, lanes] * right[k]
                        for i in range(STEP)
                        for (k, left), total in zip(
                            enumerate((own_ab, own_b, own_a)), sums[3 * i : 3 * i + 3]
                        )
                    )

                zeros = jnp.zeros((HALF, LANES), jnp.float32)
                sums = lax.fori_loop(0, spec_count, add, (zeros,) * (3 * STEP), unroll=4)
                for i in range(STEP):
                    out_ref[0, 0, near + i, some, lanes] = sums[3 * i] - sums[3 * i + 1]
                    out_ref[0, 1, near + i, some, lanes] = sums[3 * i] - sums[3 * i + 2]


def correlate(own, far, offset, table, held):
    spec_count, ants, width = own.shape
    channels = width // 2
    tiles = table.shape[0]
    slot = lambda w: sum(jnp.where(w[t] == offset, t, 0) for t in range(1, tiles))
    shape = (tiles, 2, ants, ants, channels)
    first = held is None
    inputs = pl.BlockSpec((spec_count, ants, width), lambda i, w: (0, 0, 0))
    return pl.pallas_call(
        functools.partial(correlate_kernel, spec_count, first),
        out_shape=jax.ShapeDtypeStruct(shape, jnp.float32),
        grid_spec=pltpu.PrefetchScalarGridSpec(
            num_scalar_prefetch=1,
            grid=(ants // ROWS,),
            in_specs=[inputs, inputs] + ([] if first else [pl.BlockSpec(memory_space=pl.ANY)]),
            out_specs=pl.BlockSpec(
                (1, 2, ROWS, ants, channels), lambda i, w: (slot(w), 0, i, 0, 0)
            ),
            scratch_shapes=[
                pltpu.VMEM((ants // ROWS, spec_count, ROWS, channels), jnp.float32)
            ] * 3
            + [pltpu.VMEM((spec_count, ants, channels), jnp.float32)] * 3,
        ),
        input_output_aliases={} if first else {3: 0},
        cost_estimate=pl.CostEstimate(
            flops=4000000000, bytes_accessed=8 * ants * ants * channels, transcendentals=0
        ),
        compiler_params=pltpu.CompilerParams(vmem_limit_bytes=GRANT),
        name="correlate",
    )(table, own, far, *([] if first else [held]))


def from_ahead(array, axis, by):
    peers = lax.axis_size(axis)
    return lax.ppermute(array, axis, [((i + by) % peers, i) for i in range(peers)])


def body(samples, tail, taps, tile_table):
    parts = lax.axis_size("tm")
    me = lax.axis_index("tm").astype(jnp.int32)
    pieces = [samples] + [from_ahead(samples, "tm", k) for k in range(1, parts)]
    spectra = channelize(pieces, tail, taps, me)
    ants = samples.shape[0]
    own = spectra.reshape(-1, ants, spectra.shape[1])
    one = from_ahead(own, "inp", 1)
    three = from_ahead(own, "inp", 3)
    held = correlate(own, own, 0, tile_table[0], None)
    held = correlate(own, one, 1, tile_table[0], held)
    three, held = lax.optimization_barrier((three, held))
    peers = lax.axis_size("inp")
    even = lax.rem(lax.axis_index("inp"), 2) == 0
    two = lax.ppermute(
        jnp.where(even, three, one), "inp", [(i, i ^ 1) for i in range(peers)]
    )
    held = correlate(own, three, 3, tile_table[0], held)
    held = correlate(own, two, 2, tile_table[0], held)
    return held[None]


def solution(mesh):
    in_specs = (P("inp", "tm"), P("inp", None), P(), P("inp", None))
    out_specs = P("inp", None, None, None, None, "tm")
    return jax.shard_map(body, mesh=mesh, in_specs=in_specs, out_specs=out_specs, check_vma=False)
```
